32 devices in a mesh: dp: 2 (over x), expert: 16 (over z, y, core).
Axes of the slice: x: 2, y: 2, z: 4, core: 2. Of those that a mesh axis runs over, the one named last changes fastest.
Arguments:
- tokens: bfloat16 [512, 4096], P('expert'), may hold values from -6 to 6
- expert_ids: int32 [512, 8], P('expert'), may hold values from 0 to 15, all different within a row; in each aligned block of 32 rows (0 to 31, 32 to 63, ...) at most 24 rows name the same one
- gate_ints: int32 [512, 8], P('expert'), may hold values from 1 to 1024
- w_gate: bfloat16 [16, 4096, 1536], P('expert', None, 'dp'), may hold values from -0.09375 to 0.09375
- w_up: bfloat16 [16, 4096, 1536], P('expert', None, 'dp'), may hold values from -0.09375 to 0.09375
- w_down: bfloat16 [16, 1536, 4096], P('expert', 'dp'), may hold values from -0.15625 to 0.15625
Outputs:
- mixed: bfloat16 [512, 4096], P('expert')
The draws below stay inside these ranges and needn't reach their ends.
Inputs may be any that keep to these rules, and one draw needn't show every extreme that they name: `expert_ids`: within the rows of one device each expert is named at most 24 times, and each row names 8 different experts.
All inputs are finite; a program needn't handle non-finite values.
Results may differ from the reference program's by a relative error of at most 0.017.
Values may be sent and summed in bfloat16 or wider, within the bound.
A program may use at most 64 MiB of HBM per device.

```python
import math
import jax
import jax.numpy as jnp
import numpy as np
from jax import lax

D = 4096
FF = 1536
TOP = 8
TOK_DEV = 32
EXPERTS = 16
TOKENS = 512
CAP = 24
N_DP = 2
N_EXPERT = 16


def touch_ends(entries, rng, least, high):
    place = [jax.random.randint(jax.random.fold_in(rng, axis), (), 0, length) for axis, length in enumerate(entries.shape)]
    longest = entries.shape.index(max(entries.shape))
    next_to = place[:longest] + [(place[longest] + 1) % entries.shape[longest]] + place[longest + 1:]
    return entries.at[tuple(place)].set(least).at[tuple(next_to)].set(high)


def shard_levels(key, shape, shards, least, high):
    def one(axis_at, shards_of):
        heights = jax.random.uniform(jax.random.fold_in(jax.random.fold_in(key, 6), axis_at), (shards_of,), jnp.float32, least / len(shards), high / len(shards))
        return jnp.repeat(jnp.exp(heights), shape[axis_at] // shards_of).reshape((-1,) + (1,) * (len(shape) - axis_at - 1))

    loudness = one(*shards[0])
    for cut in shards[1:]:
        loudness = loudness * one(*cut)
    return loudness


def assign_block(stream_key, own, number, rows, count, top, bound, skew):
    ranking = jax.random.permutation(stream_key, count)
    heavy_load, usual = portions_of(count, rows * top, bound, skew, True), portions_of(count, rows * top, bound, skew, False)
    places = jnp.arange(count)

    def named(sizes, offset_by):
        used = int((sizes > 0).sum())
        fixed = max(1, used // 4)
        shifted = fixed + (places - fixed + offset_by * (used - fixed)) % max(1, count - fixed)
        return jnp.zeros((count,), jnp.int32).at[ranking[jnp.where(places < fixed, places, shifted)]].set(jnp.asarray(sizes, jnp.int32))

    sizes = jnp.where(number % 4 == 0, named(heavy_load, number // 4), named(usual, number - number // 4 - 1))
    mixed = jax.random.permutation(jax.random.fold_in(own, 3), count)
    giver, sink = mixed[0:count // 2 * 2:2], mixed[1:count // 2 * 2:2]
    room = jnp.minimum(sizes[giver] - 1, bound - sizes[sink]) // 2
    room = jnp.where((giver == ranking[0]) | (sink == ranking[0]) | (sizes[sink] == 0), 0, jnp.maximum(room, 0))
    shifted = jax.random.randint(jax.random.fold_in(own, 4), (count // 2,), 0, 1 << 20) % (room + 1)
    sizes = sizes.at[giver].add(-shifted).at[sink].add(shifted)
    members = jnp.searchsorted(jnp.cumsum(sizes), jnp.arange(rows * top), side="right").astype(jnp.int32)
    listing = members.reshape(top, rows).T
    listing = listing[jax.random.permutation(jax.random.fold_in(own, 1), rows)]
    offset_by = jax.random.randint(jax.random.fold_in(own, 2), (rows, 1), 0, top)
    return jnp.take_along_axis(listing, (jnp.arange(top)[None, :] + offset_by) % top, axis=1)


def portions_of(number_of, total, reach, slope, full):
    portions = [(1 << 20) // math.isqrt(standing ** slope) + 1 for standing in range(1, number_of + 1)]
    largest = reach if full else min(reach, max(-(-total // number_of), total * portions[0] // sum(portions)))
    least = 1 if total - largest >= number_of - 1 else 0
    holding, rest = [largest] + [least] * (number_of - 1), total - largest - least * (number_of - 1)
    while rest > 0:
        candidates = [i for i in range(1, number_of) if holding[i] < largest] or [i for i in range(1, number_of) if holding[i] < reach]
        whole, budget = sum([portions[i] for i in candidates]), rest
        for i in candidates:
            addition = min(reach - holding[i], max(1, budget * portions[i] // whole), rest)
            holding[i] = holding[i] + addition
            rest = rest - addition
    return np.array(holding)


def noise(stream_key, shape, deviation, most, shards=(), kind=jnp.bfloat16):
    values = jax.random.normal(stream_key, shape, jnp.float32) * deviation
    if len(shards) > 0:
        values = shard_levels(stream_key, shape, shards, -0.22, 0.18) * values
    return jnp.clip(values, min=-most, max=most).astype(kind)


def setup_inputs(seed: int = 0) -> dict:
    arg_keys = jax.random.split(jax.random.key(seed), 7)
    tokens = noise(arg_keys[0], (TOKENS, D), 1.0, 6.0, ((0, 16),))
    expert_ids_keys = jax.random.split(jax.random.fold_in(arg_keys[1], 1), TOKENS // TOK_DEV)
    expert_ids_turns = jax.random.permutation(jax.random.fold_in(arg_keys[1], 3), TOKENS // TOK_DEV)
    expert_ids = jax.vmap(lambda own, number: assign_block(jax.random.fold_in(arg_keys[1], 2), own, number, TOK_DEV, EXPERTS, TOP, CAP, 2))(expert_ids_keys, expert_ids_turns).reshape((TOKENS, TOP))
    gate_ints = touch_ends(jax.random.randint(arg_keys[2], (TOKENS, TOP), 1, 1025), jax.random.fold_in(arg_keys[2], 1), 1, 1024).astype(jnp.int32)
    w_gate = noise(arg_keys[3], (EXPERTS, D, FF), D ** -0.5, 0.09375, ((0, 16), (2, 2)))
    w_up = noise(arg_keys[4], (EXPERTS, D, FF), D ** -0.5, 0.09375, ((0, 16), (2, 2)))
    w_down = noise(arg_keys[5], (EXPERTS, FF, D), FF ** -0.5, 0.15625, ((0, 16), (1, 2)))
    return dict(tokens=tokens, expert_ids=expert_ids, gate_ints=gate_ints, w_gate=w_gate, w_up=w_up, w_down=w_down)


def slots_of(expert_ids):
    blocks = expert_ids.reshape(N_EXPERT, TOK_DEV * TOP)
    onehot = (blocks[:, :, None] == jnp.arange(EXPERTS, dtype=jnp.int32)[None, None, :]).astype(jnp.int32)
    before = jnp.cumsum(onehot, axis=1) - onehot
    slot = jnp.sum(before * onehot, axis=2)
    return slot.reshape(TOKENS, TOP).astype(jnp.int32)


def expert_forward(packed):
    rows, gate_w, up_w, down_w = packed
    gate = jnp.dot(rows, gate_w, preferred_element_type=jnp.float32)
    up = jnp.dot(rows, up_w, preferred_element_type=jnp.float32)
    hidden = (jax.nn.silu(gate) * up).astype(jnp.bfloat16)
    split_hidden = hidden.reshape(rows.shape[0], N_DP, FF // N_DP).astype(jnp.float32)
    split_down = down_w.reshape(N_DP, FF // N_DP, D).astype(jnp.float32)
    partial_value = jnp.einsum("rsf,sfd->srd", split_hidden, split_down)
    partial_value = lax.optimization_barrier(partial_value.astype(jnp.bfloat16))
    return jnp.sum(partial_value.astype(jnp.float32), axis=0)


def reference(tokens, expert_ids, gate_ints, w_gate, w_up, w_down):
    slot = slots_of(expert_ids)
    block = (jnp.arange(TOKENS, dtype=jnp.int32) // TOK_DEV)[:, None]
    row_index = (block * CAP + slot).astype(jnp.int32)
    token_rows = jnp.broadcast_to(tokens[:, None, :], (TOKENS, TOP, D))
    buffer = jnp.zeros((EXPERTS, N_EXPERT * CAP, D), jnp.bfloat16)
    buffer = buffer.at[expert_ids.reshape(-1), row_index.reshape(-1)].set(token_rows.reshape(-1, D))
    expert_out = lax.map(expert_forward, (buffer, w_gate, w_up, w_down))
    picked = expert_out[expert_ids.reshape(-1), row_index.reshape(-1)].reshape(TOKENS, TOP, D)
    weights = gate_ints.astype(jnp.float32) / 1024.0
    mixed = jnp.sum(weights[:, :, None] * picked, axis=1)
    return mixed.astype(jnp.bfloat16)
```

```python
import jax
import jax.numpy as jnp
from jax import lax
from jax.sharding import PartitionSpec as P


def dispatch_form(tokens, expert_ids, gate_ints, w_gate, w_up, w_down):
    tok_rows = tokens.shape[0]
    top_count = expert_ids.shape[1]
    feature = tokens.shape[1]
    groups = lax.axis_size("expert")
    capacity = min(tok_rows, max(2, 3 * tok_rows * top_count // (2 * groups)))
    pairs = tok_rows * top_count
    flat_ids = expert_ids.reshape(pairs)
    onehot = (flat_ids[:, None] == jnp.arange(groups, dtype=jnp.int32)[None, :]).astype(jnp.int32)
    before = jnp.cumsum(onehot, axis=0) - onehot
    slot = jnp.sum(before * onehot, axis=1)
    target = flat_ids * capacity + slot
    select = (jnp.arange(groups * capacity, dtype=jnp.int32)[:, None] == target[None, :]).astype(
        jnp.bfloat16
    )
    owner = (
        (jnp.arange(pairs, dtype=jnp.int32) // top_count)[:, None]
        == jnp.arange(tok_rows, dtype=jnp.int32)[None, :]
    ).astype(jnp.bfloat16)
    placing = jnp.dot(select, owner, preferred_element_type=jnp.float32).astype(jnp.bfloat16)
    outgoing = jnp.dot(placing, tokens, preferred_element_type=jnp.float32).astype(jnp.bfloat16)
    arrived = lax.all_to_all(
        outgoing.reshape(groups, capacity, feature),
        "expert",
        split_axis=0,
        concat_axis=0,
        tiled=True,
    )
    rows = arrived.reshape(groups * capacity, feature)
    gate = jnp.dot(rows, w_gate[0], preferred_element_type=jnp.float32)
    up = jnp.dot(rows, w_up[0], preferred_element_type=jnp.float32)
    hidden = (jax.nn.silu(gate) * up).astype(jnp.bfloat16)
    partial_value = jnp.dot(hidden, w_down[0], preferred_element_type=jnp.float32).astype(
        jnp.bfloat16
    )
    back = lax.all_to_all(
        partial_value.reshape(groups, capacity, feature),
        "expert",
        split_axis=0,
        concat_axis=0,
        tiled=True,
    )
    back_rows = back.reshape(groups * capacity, feature)
    weights = (gate_ints.astype(jnp.float32) / 1024.0)[:, :, None]
    picked = (
        jnp.take(back_rows, target, axis=0)
        .reshape(tok_rows, top_count, feature)
        .astype(jnp.float32)
    )
    local_mix = jnp.sum(weights * picked, axis=1)
    mixed = lax.psum(local_mix.astype(jnp.bfloat16), "dp")
    return mixed


def dense_form(tokens, expert_ids, gate_ints, w_gate, w_up, w_down):
    groups = lax.axis_size("expert")
    me = lax.axis_index("expert")
    chosen = expert_ids[:, :, None] == jnp.arange(groups, dtype=jnp.int32)[None, None, :]
    coef = jnp.sum(jnp.where(chosen, gate_ints[:, :, None], 0), axis=1).astype(jnp.float32) / 1024.0
    rows = lax.all_gather(tokens, "expert", axis=0, tiled=True)
    coefs = lax.all_gather(coef, "expert", axis=0, tiled=True)
    mine = lax.dynamic_slice_in_dim(coefs, me, 1, axis=1)
    gate = jnp.dot(rows, w_gate[0], preferred_element_type=jnp.float32)
    up = jnp.dot(rows, w_up[0], preferred_element_type=jnp.float32)
    hidden = (jax.nn.silu(gate) * up).astype(jnp.bfloat16)
    part = mine * jnp.dot(hidden, w_down[0], preferred_element_type=jnp.float32)
    local = lax.psum_scatter(part.astype(jnp.bfloat16), "expert", scatter_dimension=0, tiled=True)
    return lax.psum(local, "dp")


def on_device(tokens, expert_ids, *rest):
    tok_rows, top_count = expert_ids.shape
    groups = lax.axis_size("expert")
    capacity = min(tok_rows, max(2, 3 * tok_rows * top_count // (2 * groups)))
    form = dense_form if tok_rows <= 2 * capacity else dispatch_form
    return form(tokens, expert_ids, *rest)


def solution(mesh):
    return jax.shard_map(
        on_device,
        mesh=mesh,
        in_specs=(
            P("expert", None),
            P("expert", None),
            P("expert", None),
            P("expert", None, "dp"),
            P("expert", None, "dp"),
            P("expert", "dp", None),
        ),
        out_specs=P("expert", None),
        check_vma=False,
    )
```

```python
import functools

import jax
import jax.numpy as jnp
from jax import lax
from jax.experimental import pallas as pl
from jax.experimental.pallas import tpu as pltpu
from jax.sharding import PartitionSpec as P

LANES = 128
CHUNKS = 4
WEIGHT_PIECES = 4


def ring_kernel(
    groups, x_ref, wg_any, wu_any, wd_any, o_ref,
    xall, wg, wu, wd, hid, part, quad, outgo, income, fin, other,
    w_sem, own_sem, ag_send, ag_recv, core_send, core_recv,
    quad_send, quad_recv, rs_send, rs_recv, dp_send, dp_recv,
):
    chips = groups // 2
    half = chips // 2
    block = x_ref.shape[0]
    width = x_ref.shape[1]
    feature = wg.shape[0]
    hidden = wg.shape[1]
    split = feature // 2
    side = chips * block

    me = lax.axis_index("expert")
    plane = lax.axis_index("dp")
    core = lax.rem(me, 2)
    chip = lax.div(me, 2)
    row, column = lax.rem(chip, 2), lax.div(chip, 2)
    place = (1 - row) * column + row * (chips - 1 - column)

    def expert_at(position):
        back = lax.div(position, half)
        there = (1 - back) * (2 * position) + back * (2 * (chips - 1 - position) + 1)
        return there * 2 + core

    right = {"expert": expert_at(lax.rem(place + 1, chips))}
    left = {"expert": expert_at(lax.rem(place + chips - 1, chips))}
    mate = {"expert": chip * 2 + (1 - core)}
    twin = {"dp": 1 - plane}
    sides = (right, left)

    def send(src, dst, send_sem, recv_sem, device):
        return pltpu.make_async_remote_copy(
            src_ref=src, dst_ref=dst, send_sem=send_sem, recv_sem=recv_sem,
            device_id=device, device_id_type=pl.DeviceIdType.MESH,
        )

    def local(index, src, dst):
        rows = src.shape[1] // WEIGHT_PIECES
        return [
            pltpu.make_async_copy(
                src.at[0, pl.ds(i * rows, rows)], dst.at[pl.ds(i * rows, rows)],
                w_sem.at[index * WEIGHT_PIECES + i],
            )
            for i in range(WEIGHT_PIECES)
        ]

    loads = [local(0, wg_any, wg), local(1, wu_any, wu), local(2, wd_any, wd)]
    own = pltpu.make_async_copy(x_ref, xall.at[pl.ds(0, block)], own_sem)
    own.start()
    for pieces in loads[:2]:
        for piece in pieces:
            piece.start()

    barrier = pltpu.get_barrier_semaphore()
    for device in (right, left, mate, twin):
        pl.semaphore_signal(barrier, inc=1, device_id=device, device_id_type=pl.DeviceIdType.MESH)
    pl.semaphore_wait(barrier, 4)

    def rows_of(slot, which):
        return pl.ds((2 * slot + which) * block, block)

    def hop(way, step):
        slot = 2 * step - 1 + way if step < half else chips - 1
        columns = pl.ds(0, width) if step < half else (pl.ds(0, split), pl.ds(split, width - split))[way]
        source = x_ref if step == 1 else xall.at[rows_of(2 * (step - 1) - 1 + way, 0)]
        return send(
            source.at[:, columns], xall.at[rows_of(slot, 0), columns],
            ag_send.at[way * half + step - 1], ag_recv.at[way * half + step - 1], sides[way],
        )

    def share(slot, way=0):
        index = slot + way
        columns = pl.ds(0, width)
        if slot == chips - 1:
            columns = (pl.ds(0, split), pl.ds(split, width - split))[way]
        source = x_ref if slot == 0 else xall.at[rows_of(slot, 0)]
        return send(
            source.at[:, columns], xall.at[rows_of(slot, 1), columns],
            core_send.at[index], core_recv.at[index], mate,
        )

    hops = [[hop(way, step) for step in range(1, half + 1)] for way in range(2)]
    shares = [share(slot) for slot in range(chips)] + [share(chips - 1, 1)]

    hops[0][0].start()
    hops[1][0].start()
    shares[0].start()

    tile = 256 if hidden % 256 == 0 else LANES

    def expert_rows(first, count):
        rows = pl.ds(2 * first * block, 2 * count * block)
        marks = xall[rows, pl.ds(feature, width - feature)].astype(jnp.float32)
        lane = lax.broadcasted_iota(jnp.int32, marks.shape, 1)
        mine = jnp.logical_or(lane == me, lane == me + groups)
        coef = jnp.sum(jnp.where(mine, marks, 0.0), axis=1, keepdims=True)

        def body(t, carry):
            columns = pl.ds(pl.multiple_of(t * tile, tile), tile)
            values = xall[rows, pl.ds(0, feature)]
            gate = jnp.dot(values, wg[:, columns], preferred_element_type=jnp.float32)
            up = jnp.dot(values, wu[:, columns], preferred_element_type=jnp.float32)
            out = (gate / (1.0 + jnp.exp(-gate)) * up * coef).astype(jnp.bfloat16)
            for slot in range(count):
                for which in range(2):
                    start = (2 * slot + which) * block
                    hid[pl.ds(which * side + (first + slot) * block, block), columns] = out[
                        start : start + block
                    ]
            return carry

        lax.fori_loop(0, hidden // tile, body, 0)

    own.wait()
    for step in range(1, half + 1):
        for way in range(2):
            hops[way][step - 1].wait_recv()
            if step < half:
                hops[way][step].start()
                shares[2 * step - 1 + way].start()
            else:
                shares[chips - 1 + way].start()
        if step == 1:
            for pieces in loads[:2]:
                for piece in pieces:
                    piece.wait()
            for piece in loads[2]:
                piece.start()
            shares[0].wait_recv()
            expert_rows(0, 1)
        else:
            shares[2 * step - 3].wait_recv()
            shares[2 * step - 2].wait_recv()
            expert_rows(2 * step - 3, 2)
    shares[chips - 1].wait_recv()
    shares[chips].wait_recv()
    expert_rows(chips - 1, 1)
    for piece in loads[2]:
        piece.wait()

    span = feature // CHUNKS
    part_tile = 256 if span % 256 == 0 else LANES

    def project(chunk, which):
        def body(t, carry):
            columns = pl.ds(pl.multiple_of(chunk * span + t * part_tile, part_tile), part_tile)
            part[pl.ds(which * side, side), columns] = jnp.dot(
                hid[pl.ds(which * side, side), :], wd[:, columns],
                preferred_element_type=jnp.float32,
            ).astype(jnp.bfloat16)
            return carry

        lax.fori_loop(0, span // part_tile, body, 0)

    def area(chunk):
        return pl.ds(chunk * span, span)

    def trade(chunk):
        return send(
            part.at[pl.ds(side, side), area(chunk)], quad.at[:, area(chunk)],
            quad_send.at[chunk], quad_recv.at[chunk], mate,
        )

    def sums(slot, columns):
        rows = pl.ds(slot * block, block)
        return part[rows, columns].astype(jnp.float32) + quad[rows, columns].astype(jnp.float32)

    def lot(way, reach):
        return pl.ds((way * half + reach - 1) * block, block)

    def ship(chunk, way, reach):
        columns = area(chunk)
        if reach == half:
            columns = pl.ds(chunk * span + way * (span // 2), span // 2)
        index = (way * half + reach - 1) * CHUNKS + chunk
        return send(
            outgo.at[lot(way, reach), columns], income.at[lot(way, reach), columns],
            rs_send.at[index], rs_recv.at[index], sides[way],
        )

    def swap(chunk):
        return send(
            fin.at[:, area(chunk)], other.at[:, area(chunk)],
            dp_send.at[chunk], dp_recv.at[chunk], twin,
        )

    trades = [trade(chunk) for chunk in range(CHUNKS)]
    swaps = [swap(chunk) for chunk in range(CHUNKS)]
    ships = {
        (chunk, way, reach): ship(chunk, way, reach)
        for chunk in range(CHUNKS) for way in range(2) for reach in range(1, half + 1)
    }

    def stage(chunk, number):
        begin = chunk * span
        if number == 0:
            project(chunk, 1)
            trades[chunk].start()
            project(chunk, 0)
        elif number == 1:
            trades[chunk].wait_recv()
            for way in range(2):
                columns = pl.ds(begin + way * (span // 2), span // 2)
                outgo[lot(way, half), columns] = sums(chips - 1, columns).astype(jnp.bfloat16)
                ships[chunk, way, half].start()
        elif number <= half:
            reach = half + 1 - number
            for way in range(2):
                ships[chunk, way, reach + 1].wait_recv()
                slot = 2 * reach - way
                for piece in range(2):
                    columns = pl.ds(begin + piece * (span // 2), span // 2)
                    total = sums(slot, columns)
                    if reach + 1 < half or piece == way:
                        total = total + income[lot(way, reach + 1), columns].astype(jnp.float32)
                    outgo[lot(way, reach), columns] = total.astype(jnp.bfloat16)
                ships[chunk, way, reach].start()
        elif number == half + 1:
            ships[chunk, 0, 1].wait_recv()
            ships[chunk, 1, 1].wait_recv()
            columns = area(chunk)
            total = sums(0, columns)
            total = total + income[lot(0, 1), columns].astype(jnp.float32)
            total = total + income[lot(1, 1), columns].astype(jnp.float32)
            fin[:, columns] = total.astype(jnp.bfloat16)
            swaps[chunk].start()
        else:
            swaps[chunk].wait_recv()
            columns = area(chunk)
            o_ref[:, columns] = (
                fin[:, columns].astype(jnp.float32) + other[:, columns].astype(jnp.float32)
            ).astype(jnp.bfloat16)

    stages = half + 3
    for wave in range(CHUNKS + stages - 1):
        if wave < CHUNKS:
            stage(wave, 0)
        for chunk in range(CHUNKS):
            if 0 < wave - chunk < stages:
                stage(chunk, wave - chunk)

    for copy in hops[0] + hops[1] + shares + trades + swaps + list(ships.values()):
        copy.wait_send()


def ring_form(tokens, expert_ids, gate_ints, w_gate, w_up, w_down):
    groups = lax.axis_size("expert")
    chips, half = groups // 2, groups // 4
    block, feature = tokens.shape
    hidden = w_gate.shape[2]
    marks = -(-2 * groups // LANES) * LANES
    lane = jnp.arange(marks, dtype=jnp.int32)[None, None, :]
    high = gate_ints // 8 * 8
    low = gate_ints - high
    ids = expert_ids[:, :, None]
    coef = jnp.sum(
        jnp.where(ids == lane, high[:, :, None], 0)
        + jnp.where(ids + groups == lane, low[:, :, None], 0),
        axis=1,
    )
    coef = (coef.astype(jnp.float32) / 1024.0).astype(jnp.bfloat16)
    x = jnp.concatenate([tokens, coef], axis=1)
    width = feature + marks
    rows = groups * block
    dma = pltpu.SemaphoreType.DMA
    return pl.pallas_call(
        functools.partial(ring_kernel, groups),
        out_shape=jax.ShapeDtypeStruct((block, feature), jnp.bfloat16),
        in_specs=[pl.BlockSpec(memory_space=pltpu.VMEM)] + [pl.BlockSpec(memory_space=pl.ANY)] * 3,
        out_specs=pl.BlockSpec(memory_space=pltpu.VMEM),
        scratch_shapes=[
            pltpu.VMEM((rows, width), jnp.bfloat16),
            pltpu.VMEM((feature, hidden), jnp.bfloat16),
            pltpu.VMEM((feature, hidden), jnp.bfloat16),
            pltpu.VMEM((hidden, feature), jnp.bfloat16),
            pltpu.VMEM((rows, hidden), jnp.bfloat16),
            pltpu.VMEM((rows, feature), jnp.bfloat16),
            pltpu.VMEM((chips * block, feature), jnp.bfloat16),
            pltpu.VMEM((2 * half * block, feature), jnp.bfloat16),
            pltpu.VMEM((2 * half * block, feature), jnp.bfloat16),
            pltpu.VMEM((block, feature), jnp.bfloat16),
            pltpu.VMEM((block, feature), jnp.bfloat16),
            dma((3 * WEIGHT_PIECES,)),
            dma,
            dma((2 * half,)),
            dma((2 * half,)),
            dma((chips + 1,)),
            dma((chips + 1,)),
            dma((CHUNKS,)),
            dma((CHUNKS,)),
            dma((2 * half * CHUNKS,)),
            dma((2 * half * CHUNKS,)),
            dma((CHUNKS,)),
            dma((CHUNKS,)),
        ],
        compiler_params=pltpu.CompilerParams(
            collective_id=0, has_side_effects=True, vmem_limit_bytes=60 * 1024 * 1024
        ),
    )(x, w_gate, w_up, w_down)


def dispatch_form(tokens, expert_ids, gate_ints, w_gate, w_up, w_down):
    tok_rows = tokens.shape[0]
    top_count = expert_ids.shape[1]
    feature = tokens.shape[1]
    groups = lax.axis_size("expert")
    capacity = min(tok_rows, max(2, 3 * tok_rows * top_count // (2 * groups)))
    pairs = tok_rows * top_count
    flat_ids = expert_ids.reshape(pairs)
    onehot = (flat_ids[:, None] == jnp.arange(groups, dtype=jnp.int32)[None, :]).astype(jnp.int32)
    before = jnp.cumsum(onehot, axis=0) - onehot
    slot = jnp.sum(before * onehot, axis=1)
    target = flat_ids * capacity + slot
    select = (jnp.arange(groups * capacity, dtype=jnp.int32)[:, None] == target[None, :]).astype(
        jnp.bfloat16
    )
    owner = (
        (jnp.arange(pairs, dtype=jnp.int32) // top_count)[:, None]
        == jnp.arange(tok_rows, dtype=jnp.int32)[None, :]
    ).astype(jnp.bfloat16)
    placing = jnp.dot(select, owner, preferred_element_type=jnp.float32).astype(jnp.bfloat16)
    outgoing = jnp.dot(placing, tokens, preferred_element_type=jnp.float32).astype(jnp.bfloat16)
    arrived = lax.all_to_all(
        outgoing.reshape(groups, capacity, feature),
        "expert",
        split_axis=0,
        concat_axis=0,
        tiled=True,
    )
    rows = arrived.reshape(groups * capacity, feature)
    gate = jnp.dot(rows, w_gate[0], preferred_element_type=jnp.float32)
    up = jnp.dot(rows, w_up[0], preferred_element_type=jnp.float32)
    hidden = (jax.nn.silu(gate) * up).astype(jnp.bfloat16)
    partial_value = jnp.dot(hidden, w_down[0], preferred_element_type=jnp.float32).astype(
        jnp.bfloat16
    )
    back = lax.all_to_all(
        partial_value.reshape(groups, capacity, feature),
        "expert",
        split_axis=0,
        concat_axis=0,
        tiled=True,
    )
    back_rows = back.reshape(groups * capacity, feature)
    weights = (gate_ints.astype(jnp.float32) / 1024.0)[:, :, None]
    picked = (
        jnp.take(back_rows, target, axis=0)
        .reshape(tok_rows, top_count, feature)
        .astype(jnp.float32)
    )
    local_mix = jnp.sum(weights * picked, axis=1)
    mixed = lax.psum(local_mix.astype(jnp.bfloat16), "dp")
    return mixed


def on_device(tokens, expert_ids, *rest):
    tok_rows, top_count = expert_ids.shape
    groups = lax.axis_size("expert")
    capacity = min(tok_rows, max(2, 3 * tok_rows * top_count // (2 * groups)))
    fits = groups % 4 == 0 and groups >= 8 and lax.axis_size("dp") == 2
    form = ring_form if fits and tok_rows <= 2 * capacity else dispatch_form
    return form(tokens, expert_ids, *rest)


def solution(mesh):
    return jax.shard_map(
        on_device,
        mesh=mesh,
        in_specs=(
            P("expert", None),
            P("expert", None),
            P("expert", None),
            P("expert", None, "dp"),
            P("expert", None, "dp"),
            P("expert", "dp", None),
        ),
        out_specs=P("expert", None),
        check_vma=False,
    )
```

```python
import functools

import jax
import jax.numpy as jnp
from jax import lax
from jax.experimental import pallas as pl
from jax.experimental.pallas import tpu as pltpu
from jax.sharding import PartitionSpec as P

LANES = 128
CHUNKS = 4
PIECES = 2
WEIGHT_PIECES = 4


def ring_kernel(
    groups, x_any, ids_ref, gates_ref, wg_any, wu_any, wd_any, o_ref,
    xall, wg, wu, wd, hid, part, quad, outgo, income, fin, other,
    w_sem, own_sem, ag_send, ag_recv, core_send, core_recv,
    quad_send, quad_recv, rs_send, rs_recv, dp_send, dp_recv,
):
    chips = groups // 2
    half = chips // 2
    block = x_any.shape[0]
    width = xall.shape[1]
    feature = wg.shape[0]
    hidden = wg.shape[1]
    side = chips * block

    me = lax.axis_index("expert")
    plane = lax.axis_index("dp")
    core = lax.rem(me, 2)
    chip = lax.div(me, 2)
    row, column = lax.rem(chip, 2), lax.div(chip, 2)
    place = (1 - row) * column + row * (chips - 1 - column)

    def expert_at(position):
        back = lax.div(position, half)
        there = (1 - back) * (2 * position) + back * (2 * (chips - 1 - position) + 1)
        return there * 2 + core

    right = {"expert": expert_at(lax.rem(place + 1, chips))}
    left = {"expert": expert_at(lax.rem(place + chips - 1, chips))}
    mate = {"expert": chip * 2 + (1 - core)}
    twin = {"dp": 1 - plane}
    sides = (right, left)

    def send(src, dst, send_sem, recv_sem, device):
        return pltpu.make_async_remote_copy(
            src_ref=src, dst_ref=dst, send_sem=send_sem, recv_sem=recv_sem,
            device_id=device, device_id_type=pl.DeviceIdType.MESH,
        )

    def local(index, src, dst):
        rows = src.shape[1] // WEIGHT_PIECES
        return [
            pltpu.make_async_copy(
                src.at[0, pl.ds(i * rows, rows)], dst.at[pl.ds(i * rows, rows)],
                w_sem.at[index * WEIGHT_PIECES + i],
            )
            for i in range(WEIGHT_PIECES)
        ]

    loads = [local(0, wg_any, wg), local(1, wu_any, wu), local(2, wd_any, wd)]
    own = pltpu.make_async_copy(x_any, xall.at[pl.ds(0, block), pl.ds(0, feature)], own_sem)
    own.start()
    for pieces in loads[:2]:
        for piece in pieces:
            piece.start()

    ids, gates = ids_ref[...], gates_ref[...]
    low = jnp.bitwise_and(gates, 7)
    high = gates - low
    lane = lax.broadcasted_iota(jnp.int32, (block, width - feature), 1)
    marks = jnp.zeros((block, width - feature), jnp.int32)
    for k in range(ids.shape[1]):
        chosen = ids[:, k : k + 1]
        marks = marks + jnp.where(lane == chosen, high[:, k : k + 1], 0)
        marks = marks + jnp.where(lane == chosen + groups, low[:, k : k + 1], 0)
    xall[pl.ds(0, block), pl.ds(feature, width - feature)] = (
        marks.astype(jnp.float32) / 1024.0
    ).astype(jnp.bfloat16)

    barrier = pltpu.get_barrier_semaphore()
    for device in (right, left, mate, twin):
        pl.semaphore_signal(barrier, inc=1, device_id=device, device_id_type=pl.DeviceIdType.MESH)
    pl.semaphore_wait(barrier, 4)

    def rows_of(slot, which):
        return pl.ds((2 * slot + which) * block, block)

    def columns_of(piece):
        begin = piece * (feature // PIECES)
        end = width if piece == PIECES - 1 else begin + feature // PIECES
        return pl.ds(begin, end - begin)

    def carries(way, step, piece):
        return step < half or piece // (PIECES // 2) == way

    def slot_of(way, step):
        return 0 if step == 0 else 2 * step - 1 + way if step < half else chips - 1

    def hop(way, step, piece):
        columns = columns_of(piece)
        index = (way * half + step - 1) * PIECES + piece
        return send(
            xall.at[rows_of(slot_of(way, step - 1), 0), columns],
            xall.at[rows_of(slot_of(way, step), 0), columns],
            ag_send.at[index], ag_recv.at[index], sides[way],
        )

    def share(slot, piece):
        columns = columns_of(piece)
        index = slot * PIECES + piece
        return send(
            xall.at[rows_of(slot, 0), columns], xall.at[rows_of(slot, 1), columns],
            core_send.at[index], core_recv.at[index], mate,
        )

    hops = {
        (way, step, piece): hop(way, step, piece)
        for step in range(1, half + 1) for piece in range(PIECES) for way in range(2)
        if carries(way, step, piece)
    }
    shares = {(slot, piece): share(slot, piece) for slot in range(chips) for piece in range(PIECES)}

    own.wait()
    for piece in range(PIECES):
        for way in range(2):
            hops[way, 1, piece].start()
    for piece in range(PIECES):
        shares[0, piece].start()

    def shared(slot):
        for piece in range(PIECES):
            shares[slot, piece].wait_recv()

    tile = 256 if hidden % 256 == 0 else LANES

    def expert_rows(first, count):
        rows = pl.ds(2 * first * block, 2 * count * block)
        marks = xall[rows, pl.ds(feature, width - feature)].astype(jnp.float32)
        lane = lax.broadcasted_iota(jnp.int32, marks.shape, 1)
        mine = jnp.logical_or(lane == me, lane == me + groups)
        coef = jnp.sum(jnp.where(mine, marks, 0.0), axis=1, keepdims=True)

        def body(t, carry):
            columns = pl.ds(pl.multiple_of(t * tile, tile), tile)
            values = xall[rows, pl.ds(0, feature)]
            gate = jnp.dot(values, wg[:, columns], preferred_element_type=jnp.float32)
            up = jnp.dot(values, wu[:, columns], preferred_element_type=jnp.float32)
            out = (gate / (1.0 + jnp.exp(-gate)) * up * coef).astype(jnp.bfloat16)
            for slot in range(count):
                for which in range(2):
                    start = (2 * slot + which) * block
                    hid[pl.ds(which * side + (first + slot) * block, block), columns] = out[
                        start : start + block
                    ]
            return carry

        lax.fori_loop(0, hidden // tile, body, 0)

    for step in range(1, half + 1):
        for piece in range(PIECES):
            for way in range(2):
                if (way, step, piece) in hops:
                    hops[way, step, piece].wait_recv()
                    if (way, step + 1, piece) in hops:
                        hops[way, step + 1, piece].start()
                    shares[slot_of(way, step), piece].start()
        if step == 1:
            for pieces in loads[:2]:
                for piece in pieces:
                    piece.wait()
            for piece in loads[2]:
                piece.start()
            shared(0)
            expert_rows(0, 1)
        else:
            shared(2 * step - 3)
            shared(2 * step - 2)
            expert_rows(2 * step - 3, 2)
    shared(chips - 1)
    expert_rows(chips - 1, 1)
    for piece in loads[2]:
        piece.wait()

    span = feature // CHUNKS
    part_tile = 256 if span % 256 == 0 else LANES

    def project(chunk, which):
        def body(t, carry):
            columns = pl.ds(pl.multiple_of(chunk * span + t * part_tile, part_tile), part_tile)
            part[pl.ds(which * side, side), columns] = jnp.dot(
                hid[pl.ds(which * side, side), :], wd[:, columns],
                preferred_element_type=jnp.float32,
            ).astype(jnp.bfloat16)
            return carry

        lax.fori_loop(0, span // part_tile, body, 0)

    def area(chunk):
        return pl.ds(chunk * span, span)

    def trade(chunk):
        return send(
            part.at[pl.ds(side, side), area(chunk)], quad.at[:, area(chunk)],
            quad_send.at[chunk], quad_recv.at[chunk], mate,
        )

    def sums(slot, columns):
        rows = pl.ds(slot * block, block)
        return part[rows, columns].astype(jnp.float32) + quad[rows, columns].astype(jnp.float32)

    def lot(way, reach):
        return pl.ds((way * half + reach - 1) * block, block)

    def ship(chunk, way, reach):
        columns = area(chunk)
        if reach == half:
            columns = pl.ds(chunk * span + way * (span // 2), span // 2)
        index = (way * half + reach - 1) * CHUNKS + chunk
        return send(
            outgo.at[lot(way, reach), columns], income.at[lot(way, reach), columns],
            rs_send.at[index], rs_recv.at[index], sides[way],
        )

    def swap(chunk):
        return send(
            fin.at[:, area(chunk)], other.at[:, area(chunk)],
            dp_send.at[chunk], dp_recv.at[chunk], twin,
        )

    trades = [trade(chunk) for chunk in range(CHUNKS)]
    swaps = [swap(chunk) for chunk in range(CHUNKS)]
    ships = {
        (chunk, way, reach): ship(chunk, way, reach)
        for chunk in range(CHUNKS) for way in range(2) for reach in range(1, half + 1)
    }

    def stage(chunk, number):
        begin = chunk * span
        if number == 0:
            project(chunk, 1)
            trades[chunk].start()
            project(chunk, 0)
        elif number == 1:
            trades[chunk].wait_recv()
            for way in range(2):
                columns = pl.ds(begin + way * (span // 2), span // 2)
                outgo[lot(way, half), columns] = sums(chips - 1, columns).astype(jnp.bfloat16)
                ships[chunk, way, half].start()
        elif number <= half:
            reach = half + 1 - number
            for way in range(2):
                ships[chunk, way, reach + 1].wait_recv()
                slot = 2 * reach - way
                for piece in range(2):
                    columns = pl.ds(begin + piece * (span // 2), span // 2)
                    total = sums(slot, columns)
                    if reach + 1 < half or piece == way:
                        total = total + income[lot(way, reach + 1), columns].astype(jnp.float32)
                    outgo[lot(way, reach), columns] = total.astype(jnp.bfloat16)
                ships[chunk, way, reach].start()
        elif number == half + 1:
            ships[chunk, 0, 1].wait_recv()
            ships[chunk, 1, 1].wait_recv()
            columns = area(chunk)
            total = sums(0, columns)
            total = total + income[lot(0, 1), columns].astype(jnp.float32)
            total = total + income[lot(1, 1), columns].astype(jnp.float32)
            fin[:, columns] = total.astype(jnp.bfloat16)
            swaps[chunk].start()
        else:
            swaps[chunk].wait_recv()
            columns = area(chunk)
            o_ref[:, columns] = (
                fin[:, columns].astype(jnp.float32) + other[:, columns].astype(jnp.float32)
            ).astype(jnp.bfloat16)

    stages = half + 3
    for wave in range(CHUNKS + stages - 1):
        if wave < CHUNKS:
            stage(wave, 0)
        for chunk in range(CHUNKS):
            if 0 < wave - chunk < stages:
                stage(chunk, wave - chunk)

    for copy in list(hops.values()) + list(shares.values()) + trades + swaps + list(ships.values()):
        copy.wait_send()


def ring_form(tokens, expert_ids, gate_ints, w_gate, w_up, w_down):
    groups = lax.axis_size("expert")
    chips, half = groups // 2, groups // 4
    block, feature = tokens.shape
    hidden = w_gate.shape[2]
    marks = -(-2 * groups // LANES) * LANES
    width = feature + marks
    rows = groups * block
    dma = pltpu.SemaphoreType.DMA
    return pl.pallas_call(
        functools.partial(ring_kernel, groups),
        out_shape=jax.ShapeDtypeStruct((block, feature), jnp.bfloat16),
        in_specs=[
            pl.BlockSpec(memory_space=pl.ANY),
            pl.BlockSpec(memory_space=pltpu.VMEM),
            pl.BlockSpec(memory_space=pltpu.VMEM),
        ]
        + [pl.BlockSpec(memory_space=pl.ANY)] * 3,
        out_specs=pl.BlockSpec(memory_space=pltpu.VMEM),
        scratch_shapes=[
            pltpu.VMEM((rows, width), jnp.bfloat16),
            pltpu.VMEM((feature, hidden), jnp.bfloat16),
            pltpu.VMEM((feature, hidden), jnp.bfloat16),
            pltpu.VMEM((hidden, feature), jnp.bfloat16),
            pltpu.VMEM((rows, hidden), jnp.bfloat16),
            pltpu.VMEM((rows, feature), jnp.bfloat16),
            pltpu.VMEM((chips * block, feature), jnp.bfloat16),
            pltpu.VMEM((2 * half * block, feature), jnp.bfloat16),
            pltpu.VMEM((2 * half * block, feature), jnp.bfloat16),
            pltpu.VMEM((block, feature), jnp.bfloat16),
            pltpu.VMEM((block, feature), jnp.bfloat16),
            dma((3 * WEIGHT_PIECES,)),
            dma,
            dma((2 * half * PIECES,)),
            dma((2 * half * PIECES,)),
            dma((chips * PIECES,)),
            dma((chips * PIECES,)),
            dma((CHUNKS,)),
            dma((CHUNKS,)),
            dma((2 * half * CHUNKS,)),
            dma((2 * half * CHUNKS,)),
            dma((CHUNKS,)),
            dma((CHUNKS,)),
        ],
        compiler_params=pltpu.CompilerParams(
            collective_id=0, has_side_effects=True, vmem_limit_bytes=60 * 1024 * 1024
        ),
    )(tokens, expert_ids, gate_ints, w_gate, w_up, w_down)


def dispatch_form(tokens, expert_ids, gate_ints, w_gate, w_up, w_down):
    tok_rows = tokens.shape[0]
    top_count = expert_ids.shape[1]
    feature = tokens.shape[1]
    groups = lax.axis_size("expert")
    capacity = min(tok_rows, max(2, 3 * tok_rows * top_count // (2 * groups)))
    pairs = tok_rows * top_count
    flat_ids = expert_ids.reshape(pairs)
    onehot = (flat_ids[:, None] == jnp.arange(groups, dtype=jnp.int32)[None, :]).astype(jnp.int32)
    before = jnp.cumsum(onehot, axis=0) - onehot
    slot = jnp.sum(before * onehot, axis=1)
    target = flat_ids * capacity + slot
    select = (jnp.arange(groups * capacity, dtype=jnp.int32)[:, None] == target[None, :]).astype(
        jnp.bfloat16
    )
    owner = (
        (jnp.arange(pairs, dtype=jnp.int32) // top_count)[:, None]
        == jnp.arange(tok_rows, dtype=jnp.int32)[None, :]
    ).astype(jnp.bfloat16)
    placing = jnp.dot(select, owner, preferred_element_type=jnp.float32).astype(jnp.bfloat16)
    outgoing = jnp.dot(placing, tokens, preferred_element_type=jnp.float32).astype(jnp.bfloat16)
    arrived = lax.all_to_all(
        outgoing.reshape(groups, capacity, feature),
        "expert",
        split_axis=0,
        concat_axis=0,
        tiled=True,
    )
    rows = arrived.reshape(groups * capacity, feature)
    gate = jnp.dot(rows, w_gate[0], preferred_element_type=jnp.float32)
    up = jnp.dot(rows, w_up[0], preferred_element_type=jnp.float32)
    hidden = (jax.nn.silu(gate) * up).astype(jnp.bfloat16)
    partial_value = jnp.dot(hidden, w_down[0], preferred_element_type=jnp.float32).astype(
        jnp.bfloat16
    )
    back = lax.all_to_all(
        partial_value.reshape(groups, capacity, feature),
        "expert",
        split_axis=0,
        concat_axis=0,
        tiled=True,
    )
    back_rows = back.reshape(groups * capacity, feature)
    weights = (gate_ints.astype(jnp.float32) / 1024.0)[:, :, None]
    picked = (
        jnp.take(back_rows, target, axis=0)
        .reshape(tok_rows, top_count, feature)
        .astype(jnp.float32)
    )
    local_mix = jnp.sum(weights * picked, axis=1)
    mixed = lax.psum(local_mix.astype(jnp.bfloat16), "dp")
    return mixed


def on_device(tokens, expert_ids, *rest):
    tok_rows, top_count = expert_ids.shape
    groups = lax.axis_size("expert")
    capacity = min(tok_rows, max(2, 3 * tok_rows * top_count // (2 * groups)))
    fits = groups % 4 == 0 and groups >= 8 and lax.axis_size("dp") == 2
    form = ring_form if fits and tok_rows <= 2 * capacity else dispatch_form
    return form(tokens, expert_ids, *rest)


def solution(mesh):
    return jax.shard_map(
        on_device,
        mesh=mesh,
        in_specs=(
            P("expert", None),
            P("expert", None),
            P("expert", None),
            P("expert", None, "dp"),
            P("expert", None, "dp"),
            P("expert", "dp", None),
        ),
        out_specs=P("expert", None),
        check_vma=False,
    )
```

```python
import functools

import jax
import jax.numpy as jnp
from jax import lax
from jax.experimental import pallas as pl
from jax.experimental.pallas import tpu as pltpu
from jax.sharding import PartitionSpec as P

LANES = 128
CHUNKS = 4
PIECES = 2
WEIGHT_PIECES = 4


def ring_kernel(
    groups, x_any, ids_ref, gates_ref, wg_any, wu_any, wd_any, o_ref,
    xall, wg, wu, wd, hid, part, quad, outgo, income, fin, other, gift, gained,
    w_sem, own_sem, ag_send, ag_recv, core_send, core_recv,
    quad_send, quad_recv, rs_send, rs_recv, dp_send, dp_recv, gift_send, gift_recv,
):
    chips = groups // 2
    half = chips // 2
    block = x_any.shape[0]
    width = xall.shape[1]
    feature = wg.shape[0]
    hidden = wg.shape[1]
    side = chips * block

    me = lax.axis_index("expert")
    plane = lax.axis_index("dp")
    core = lax.rem(me, 2)
    chip = lax.div(me, 2)
    row, column = lax.rem(chip, 2), lax.div(chip, 2)
    place = (1 - row) * column + row * (chips - 1 - column)

    def expert_at(position):
        back = lax.div(position, half)
        there = (1 - back) * (2 * position) + back * (2 * (chips - 1 - position) + 1)
        return there * 2 + core

    right = {"expert": expert_at(lax.rem(place + 1, chips))}
    left = {"expert": expert_at(lax.rem(place + chips - 1, chips))}
    mate = {"expert": chip * 2 + (1 - core)}
    twin = {"dp": 1 - plane}
    sides = (right, left)

    def send(src, dst, send_sem, recv_sem, device):
        return pltpu.make_async_remote_copy(
            src_ref=src, dst_ref=dst, send_sem=send_sem, recv_sem=recv_sem,
            device_id=device, device_id_type=pl.DeviceIdType.MESH,
        )

    def local(index, src, dst):
        rows = src.shape[1] // WEIGHT_PIECES
        return [
            pltpu.make_async_copy(
                src.at[0, pl.ds(i * rows, rows)], dst.at[pl.ds(i * rows, rows)],
                w_sem.at[index * WEIGHT_PIECES + i],
            )
            for i in range(WEIGHT_PIECES)
        ]

    loads = [local(0, wg_any, wg), local(1, wu_any, wu), local(2, wd_any, wd)]
    own = pltpu.make_async_copy(x_any, xall.at[pl.ds(0, block), pl.ds(0, feature)], own_sem)
    own.start()
    for pieces in loads[:2]:
        for piece in pieces:
            piece.start()

    ids, gates = ids_ref[...], gates_ref[...]
    low = jnp.bitwise_and(gates, 7)
    high = gates - low
    lane = lax.broadcasted_iota(jnp.int32, (block, width - feature), 1)
    marks = jnp.zeros((block, width - feature), jnp.int32)
    for k in range(ids.shape[1]):
        chosen = ids[:, k : k + 1]
        marks = marks + jnp.where(lane == chosen, high[:, k : k + 1], 0)
        marks = marks + jnp.where(lane == chosen + groups, low[:, k : k + 1], 0)
    xall[pl.ds(0, block), pl.ds(feature, width - feature)] = (
        marks.astype(jnp.float32) / 1024.0
    ).astype(jnp.bfloat16)

    barrier = pltpu.get_barrier_semaphore()
    for device in (right, left, mate, twin):
        pl.semaphore_signal(barrier, inc=1, device_id=device, device_id_type=pl.DeviceIdType.MESH)
    pl.semaphore_wait(barrier, 4)

    def rows_of(slot, which):
        return pl.ds((2 * slot + which) * block, block)

    def columns_of(piece):
        begin = piece * (feature // PIECES)
        end = width if piece == PIECES - 1 else begin + feature // PIECES
        return pl.ds(begin, end - begin)

    def carries(way, step, piece):
        return step < half or piece // (PIECES // 2) == way

    def slot_of(way, step):
        return 0 if step == 0 else 2 * step - 1 + way if step < half else chips - 1

    def hop(way, step, piece):
        columns = columns_of(piece)
        index = (way * half + step - 1) * PIECES + piece
        return send(
            xall.at[rows_of(slot_of(way, step - 1), 0), columns],
            xall.at[rows_of(slot_of(way, step), 0), columns],
            ag_send.at[index], ag_recv.at[index], sides[way],
        )

    def share(slot, piece):
        columns = columns_of(piece)
        index = slot * PIECES + piece
        return send(
            xall.at[rows_of(slot, 0), columns], xall.at[rows_of(slot, 1), columns],
            core_send.at[index], core_recv.at[index], mate,
        )

    hops = {
        (way, step, piece): hop(way, step, piece)
        for step in range(1, half + 1) for piece in range(PIECES) for way in range(2)
        if carries(way, step, piece)
    }
    shares = {(slot, piece): share(slot, piece) for slot in range(chips) for piece in range(PIECES)}

    own.wait()
    for piece in range(PIECES):
        for way in range(2):
            hops[way, 1, piece].start()
    for piece in range(PIECES):
        shares[0, piece].start()

    def shared(slot):
        for piece in range(PIECES):
            shares[slot, piece].wait_recv()

    tile = 256 if hidden % 256 == 0 else LANES

    def expert_rows(first, count):
        rows = pl.ds(2 * first * block, 2 * count * block)
        marks = xall[rows, pl.ds(feature, width - feature)].astype(jnp.float32)
        lane = lax.broadcasted_iota(jnp.int32, marks.shape, 1)
        mine = jnp.logical_or(lane == me, lane == me + groups)
        coef = jnp.sum(jnp.where(mine, marks, 0.0), axis=1, keepdims=True)

        def body(t, carry):
            columns = pl.ds(pl.multiple_of(t * tile, tile), tile)
            values = xall[rows, pl.ds(0, feature)]
            gate = jnp.dot(values, wg[:, columns], preferred_element_type=jnp.float32)
            up = jnp.dot(values, wu[:, columns], preferred_element_type=jnp.float32)
            out = (gate / (1.0 + jnp.exp(-gate)) * up * coef).astype(jnp.bfloat16)
            for slot in range(count):
                for which in range(2):
                    start = (2 * slot + which) * block
                    hid[pl.ds(which * side + (first + slot) * block, block), columns] = out[
                        start : start + block
                    ]
            return carry

        lax.fori_loop(0, hidden // tile, body, 0)

    for step in range(1, half + 1):
        for piece in range(PIECES):
            for way in range(2):
                if (way, step, piece) in hops:
                    hops[way, step, piece].wait_recv()
                    if (way, step + 1, piece) in hops:
                        hops[way, step + 1, piece].start()
                    shares[slot_of(way, step), piece].start()
        if step == 1:
            for pieces in loads[:2]:
                for piece in pieces:
                    piece.wait()
            for piece in loads[2]:
                piece.start()
            shared(0)
            expert_rows(0, 1)
        else:
            shared(2 * step - 3)
            shared(2 * step - 2)
            expert_rows(2 * step - 3, 2)
    shared(chips - 1)
    expert_rows(chips - 1, 1)
    for piece in loads[2]:
        piece.wait()

    span = feature // CHUNKS
    part_tile = 256 if span % 256 == 0 else LANES

    last = CHUNKS - 1
    starts = [(1 - plane) * (last * span)] + [k * span for k in range(1, last)] + [plane * (last * span)]

    def at(chunk, offset, count):
        begin = starts[chunk] + offset
        if chunk in (0, last):
            begin = pl.multiple_of(begin, LANES)
        return pl.ds(begin, count)

    def project(chunk, which):
        def body(t, carry):
            columns = pl.ds(pl.multiple_of(starts[chunk] + t * part_tile, part_tile), part_tile)
            part[pl.ds(which * side, side), columns] = jnp.dot(
                hid[pl.ds(which * side, side), :], wd[:, columns],
                preferred_element_type=jnp.float32,
            ).astype(jnp.bfloat16)
            return carry

        lax.fori_loop(0, span // part_tile, body, 0)

    def area(chunk):
        return at(chunk, 0, span)

    def trade(chunk):
        return send(
            part.at[pl.ds(side, side), area(chunk)], quad.at[:, area(chunk)],
            quad_send.at[chunk], quad_recv.at[chunk], mate,
        )

    def sums(chunk, slot, offset, count):
        rows, columns = pl.ds(slot * block, block), at(chunk, offset, count)
        total = part[rows, columns].astype(jnp.float32) + quad[rows, columns].astype(jnp.float32)
        if chunk == last:
            total = total + gained[rows, pl.ds(offset, count)].astype(jnp.float32)
        return total

    def give(slot):
        rows = pl.ds(slot * block, block)
        return send(
            gift.at[rows], gained.at[rows], gift_send.at[slot], gift_recv.at[slot], twin
        )

    def lot(way, reach):
        return pl.ds((way * half + reach - 1) * block, block)

    def ship(chunk, way, reach):
        columns = area(chunk)
        if reach == half:
            columns = at(chunk, way * (span // 2), span // 2)
        index = (way * half + reach - 1) * CHUNKS + chunk
        return send(
            outgo.at[lot(way, reach), columns], income.at[lot(way, reach), columns],
            rs_send.at[index], rs_recv.at[index], sides[way],
        )

    def swap(chunk):
        return send(
            fin.at[:, area(chunk)], other.at[:, area(chunk)],
            dp_send.at[chunk], dp_recv.at[chunk], twin,
        )

    gifts = [give(slot) for slot in range(chips)]
    trades = [trade(chunk) for chunk in range(CHUNKS)]
    swaps = {chunk: swap(chunk) for chunk in range(1, CHUNKS)}
    ships = {
        (chunk, way, reach): ship(chunk, way, reach)
        for chunk in range(1, CHUNKS) for way in range(2) for reach in range(1, half + 1)
    }

    def stage(chunk, number):
        if number == 0:
            project(chunk, 1)
            trades[chunk].start()
            project(chunk, 0)
        elif number == 1 and chunk == 0:
            trades[chunk].wait_recv()
            for slot in reversed(range(chips)):
                gift[pl.ds(slot * block, block), :] = sums(0, slot, 0, span).astype(jnp.bfloat16)
                gifts[slot].start()
        elif chunk == 0:
            pass
        elif number == 1:
            trades[chunk].wait_recv()
            if chunk == last:
                gifts[chips - 1].wait_recv()
            for way in range(2):
                columns = at(chunk, way * (span // 2), span // 2)
                total = sums(chunk, chips - 1, way * (span // 2), span // 2)
                outgo[lot(way, half), columns] = total.astype(jnp.bfloat16)
                ships[chunk, way, half].start()
        elif number <= half:
            reach = half + 1 - number
            for way in range(2):
                ships[chunk, way, reach + 1].wait_recv()
                slot = 2 * reach - way
                if chunk == last:
                    gifts[slot].wait_recv()
                for piece in range(2):
                    columns = at(chunk, piece * (span // 2), span // 2)
                    total = sums(chunk, slot, piece * (span // 2), span // 2)
                    if reach + 1 < half or piece == way:
                        total = total + income[lot(way, reach + 1), columns].astype(jnp.float32)
                    outgo[lot(way, reach), columns] = total.astype(jnp.bfloat16)
                ships[chunk, way, reach].start()
        elif number == half + 1:
            ships[chunk, 0, 1].wait_recv()
            ships[chunk, 1, 1].wait_recv()
            columns = area(chunk)
            if chunk == last:
                gifts[0].wait_recv()
            total = sums(chunk, 0, 0, span)
            total = total + income[lot(0, 1), columns].astype(jnp.float32)
            total = total + income[lot(1, 1), columns].astype(jnp.float32)
            fin[:, columns] = total.astype(jnp.bfloat16)
            swaps[chunk].start()
        else:
            swaps[chunk].wait_recv()
            columns = area(chunk)
            if chunk == last:
                o_ref[:, columns] = fin[:, columns]
                o_ref[:, area(0)] = other[:, area(0)]
                return
            o_ref[:, columns] = (
                fin[:, columns].astype(jnp.float32) + other[:, columns].astype(jnp.float32)
            ).astype(jnp.bfloat16)

    stages = half + 3
    for wave in range(CHUNKS + stages - 1):
        if wave < CHUNKS:
            stage(wave, 0)
        for chunk in range(CHUNKS):
            if 0 < wave - chunk < stages:
                stage(chunk, wave - chunk)

    copies = list(hops.values()) + list(shares.values()) + trades
    for copy in copies + gifts + list(swaps.values()) + list(ships.values()):
        copy.wait_send()


def ring_form(tokens, expert_ids, gate_ints, w_gate, w_up, w_down):
    groups = lax.axis_size("expert")
    chips, half = groups // 2, groups // 4
    block, feature = tokens.shape
    hidden = w_gate.shape[2]
    marks = -(-2 * groups // LANES) * LANES
    width = feature + marks
    rows = groups * block
    dma = pltpu.SemaphoreType.DMA
    return pl.pallas_call(
        functools.partial(ring_kernel, groups),
        out_shape=jax.ShapeDtypeStruct((block, feature), jnp.bfloat16),
        in_specs=[
            pl.BlockSpec(memory_space=pl.ANY),
            pl.BlockSpec(memory_space=pltpu.VMEM),
            pl.BlockSpec(memory_space=pltpu.VMEM),
        ]
        + [pl.BlockSpec(memory_space=pl.ANY)] * 3,
        out_specs=pl.BlockSpec(memory_space=pltpu.VMEM),
        scratch_shapes=[
            pltpu.VMEM((rows, width), jnp.bfloat16),
            pltpu.VMEM((feature, hidden), jnp.bfloat16),
            pltpu.VMEM((feature, hidden), jnp.bfloat16),
            pltpu.VMEM((hidden, feature), jnp.bfloat16),
            pltpu.VMEM((rows, hidden), jnp.bfloat16),
            pltpu.VMEM((rows, feature), jnp.bfloat16),
            pltpu.VMEM((chips * block, feature), jnp.bfloat16),
            pltpu.VMEM((2 * half * block, feature), jnp.bfloat16),
            pltpu.VMEM((2 * half * block, feature), jnp.bfloat16),
            pltpu.VMEM((block, feature), jnp.bfloat16),
            pltpu.VMEM((block, feature), jnp.bfloat16),
            pltpu.VMEM((chips * block, feature // CHUNKS), jnp.bfloat16),
            pltpu.VMEM((chips * block, feature // CHUNKS), jnp.bfloat16),
            dma((3 * WEIGHT_PIECES,)),
            dma,
            dma((2 * half * PIECES,)),
            dma((2 * half * PIECES,)),
            dma((chips * PIECES,)),
            dma((chips * PIECES,)),
            dma((CHUNKS,)),
            dma((CHUNKS,)),
            dma((2 * half * CHUNKS,)),
            dma((2 * half * CHUNKS,)),
            dma((CHUNKS,)),
            dma((CHUNKS,)),
            dma((chips,)),
            dma((chips,)),
        ],
        compiler_params=pltpu.CompilerParams(
            collective_id=0, has_side_effects=True, vmem_limit_bytes=60 * 1024 * 1024
        ),
    )(tokens, expert_ids, gate_ints, w_gate, w_up, w_down)


def dispatch_form(tokens, expert_ids, gate_ints, w_gate, w_up, w_down):
    tok_rows = tokens.shape[0]
    top_count = expert_ids.shape[1]
    feature = tokens.shape[1]
    groups = lax.axis_size("expert")
    capacity = min(tok_rows, max(2, 3 * tok_rows * top_count // (2 * groups)))
    pairs = tok_rows * top_count
    flat_ids = expert_ids.reshape(pairs)
    onehot = (flat_ids[:, None] == jnp.arange(groups, dtype=jnp.int32)[None, :]).astype(jnp.int32)
    before = jnp.cumsum(onehot, axis=0) - onehot
    slot = jnp.sum(before * onehot, axis=1)
    target = flat_ids * capacity + slot
    select = (jnp.arange(groups * capacity, dtype=jnp.int32)[:, None] == target[None, :]).astype(
        jnp.bfloat16
    )
    owner = (
        (jnp.arange(pairs, dtype=jnp.int32) // top_count)[:, None]
        == jnp.arange(tok_rows, dtype=jnp.int32)[None, :]
    ).astype(jnp.bfloat16)
    placing = jnp.dot(select, owner, preferred_element_type=jnp.float32).astype(jnp.bfloat16)
    outgoing = jnp.dot(placing, tokens, preferred_element_type=jnp.float32).astype(jnp.bfloat16)
    arrived = lax.all_to_all(
        outgoing.reshape(groups, capacity, feature),
        "expert",
        split_axis=0,
        concat_axis=0,
        tiled=True,
    )
    rows = arrived.reshape(groups * capacity, feature)
    gate = jnp.dot(rows, w_gate[0], preferred_element_type=jnp.float32)
    up = jnp.dot(rows, w_up[0], preferred_element_type=jnp.float32)
    hidden = (jax.nn.silu(gate) * up).astype(jnp.bfloat16)
    partial_value = jnp.dot(hidden, w_down[0], preferred_element_type=jnp.float32).astype(
        jnp.bfloat16
    )
    back = lax.all_to_all(
        partial_value.reshape(groups, capacity, feature),
        "expert",
        split_axis=0,
        concat_axis=0,
        tiled=True,
    )
    back_rows = back.reshape(groups * capacity, feature)
    weights = (gate_ints.astype(jnp.float32) / 1024.0)[:, :, None]
    picked = (
        jnp.take(back_rows, target, axis=0)
        .reshape(tok_rows, top_count, feature)
        .astype(jnp.float32)
    )
    local_mix = jnp.sum(weights * picked, axis=1)
    mixed = lax.psum(local_mix.astype(jnp.bfloat16), "dp")
    return mixed


def on_device(tokens, expert_ids, *rest):
    tok_rows, top_count = expert_ids.shape
    groups = lax.axis_size("expert")
    capacity = min(tok_rows, max(2, 3 * tok_rows * top_count // (2 * groups)))
    fits = groups % 4 == 0 and groups >= 8 and lax.axis_size("dp") == 2
    form = ring_form if fits and tok_rows <= 2 * capacity else dispatch_form
    return form(tokens, expert_ids, *rest)


def solution(mesh):
    return jax.shard_map(
        on_device,
        mesh=mesh,
        in_specs=(
            P("expert", None),
            P("expert", None),
            P("expert", None),
            P("expert", None, "dp"),
            P("expert", None, "dp"),
            P("expert", "dp", None),
        ),
        out_specs=P("expert", None),
        check_vma=False,
    )
```

```python
import functools

import jax
import jax.numpy as jnp
from jax import lax
from jax.experimental import pallas as pl
from jax.experimental.pallas import tpu as pltpu
from jax.sharding import PartitionSpec as P

LANES = 128
CHUNKS = 4
PIECES = 4
WEIGHT_PIECES = 4


def ring_kernel(
    groups, x_any, ids_ref, gates_ref, wg_any, wu_any, wd_any, o_ref,
    xall, wg, wu, wd, hid, part, quad, outgo, income, fin, other, gift, gained,
    w_sem, own_sem, ag_send, ag_recv, core_send, core_recv,
    quad_send, quad_recv, rs_send, rs_recv, dp_send, dp_recv, gift_send, gift_recv, cross_send, cross_recv,
):
    chips = groups // 2
    half = chips // 2
    block = x_any.shape[0]
    width = xall.shape[1]
    feature = wg.shape[0]
    hidden = wg.shape[1]
    side = chips * block

    me = lax.axis_index("expert")
    plane = lax.axis_index("dp")
    core = lax.rem(me, 2)
    chip = lax.div(me, 2)
    row, column = lax.rem(chip, 2), lax.div(chip, 2)
    place = (1 - row) * column + row * (chips - 1 - column)

    def expert_at(position):
        back = lax.div(position, half)
        there = (1 - back) * (2 * position) + back * (2 * (chips - 1 - position) + 1)
        return there * 2 + core

    right = {"expert": expert_at(lax.rem(place + 1, chips))}
    left = {"expert": expert_at(lax.rem(place + chips - 1, chips))}
    mate = {"expert": chip * 2 + (1 - core)}
    twin = {"dp": 1 - plane}
    sides = (right, left)

    def send(src, dst, send_sem, recv_sem, device):
        return pltpu.make_async_remote_copy(
            src_ref=src, dst_ref=dst, send_sem=send_sem, recv_sem=recv_sem,
            device_id=device, device_id_type=pl.DeviceIdType.MESH,
        )

    def local(index, src, dst):
        rows = src.shape[1] // WEIGHT_PIECES
        return [
            pltpu.make_async_copy(
                src.at[0, pl.ds(i * rows, rows)], dst.at[pl.ds(i * rows, rows)],
                w_sem.at[index * WEIGHT_PIECES + i],
            )
            for i in range(WEIGHT_PIECES)
        ]

    loads = [local(0, wg_any, wg), local(1, wu_any, wu), local(2, wd_any, wd)]
    own = pltpu.make_async_copy(x_any, xall.at[pl.ds(0, block), pl.ds(0, feature)], own_sem)
    own.start()
    for pieces in loads[:2]:
        for piece in pieces:
            piece.start()

    ids, gates = ids_ref[...], gates_ref[...]
    low = jnp.bitwise_and(gates, 7)
    high = gates - low
    lane = lax.broadcasted_iota(jnp.int32, (block, width - feature), 1)
    marks = jnp.zeros((block, width - feature), jnp.int32)
    for k in range(ids.shape[1]):
        chosen = ids[:, k : k + 1]
        marks = marks + jnp.where(lane == chosen, high[:, k : k + 1], 0)
        marks = marks + jnp.where(lane == chosen + groups, low[:, k : k + 1], 0)
    xall[pl.ds(0, block), pl.ds(feature, width - feature)] = (
        marks.astype(jnp.float32) / 1024.0
    ).astype(jnp.bfloat16)

    barrier = pltpu.get_barrier_semaphore()
    for device in (right, left, mate, twin):
        pl.semaphore_signal(barrier, inc=1, device_id=device, device_id_type=pl.DeviceIdType.MESH)
    pl.semaphore_wait(barrier, 4)

    def rows_of(slot, which):
        return pl.ds((2 * slot + which) * block, block)

    def columns_of(piece):
        if piece < 2:
            begin = (plane if piece == 0 else 1 - plane) * (feature // PIECES)
            return pl.ds(pl.multiple_of(begin, LANES), feature // PIECES)
        begin = piece * (feature // PIECES)
        end = width if piece == PIECES - 1 else begin + feature // PIECES
        return pl.ds(begin, end - begin)

    def carries(way, step, piece):
        if piece == 1:
            return False
        return step < half or (piece == PIECES - 1) == (way == 1)

    def slot_of(way, step):
        return 0 if step == 0 else 2 * step - 1 + way if step < half else chips - 1

    def hop(way, step, piece):
        columns = columns_of(piece)
        index = (way * half + step - 1) * PIECES + piece
        return send(
            xall.at[rows_of(slot_of(way, step - 1), 0), columns],
            xall.at[rows_of(slot_of(way, step), 0), columns],
            ag_send.at[index], ag_recv.at[index], sides[way],
        )

    def share(slot, piece):
        columns = columns_of(piece)
        index = slot * PIECES + piece
        return send(
            xall.at[rows_of(slot, 0), columns], xall.at[rows_of(slot, 1), columns],
            core_send.at[index], core_recv.at[index], mate,
        )

    hops = {
        (way, step, piece): hop(way, step, piece)
        for step in range(1, half + 1) for piece in range(PIECES) for way in range(2)
        if carries(way, step, piece)
    }
    shares = {(slot, piece): share(slot, piece) for slot in range(chips) for piece in range(PIECES)}

    def cross(slot):
        area = xall.at[rows_of(slot, 0), columns_of(0)]
        return send(area, area, cross_send.at[slot], cross_recv.at[slot], twin)

    crosses = {slot: cross(slot) for slot in range(1, chips)}

    def crossed(slot):
        crosses[slot].wait_recv()
        shares[slot, 1].start()

    own.wait()
    for piece in range(PIECES):
        for way in range(2):
            if (way, 1, piece) in hops:
                hops[way, 1, piece].start()
    for piece in range(PIECES):
        shares[0, piece].start()

    def shared(slot):
        for piece in range(PIECES):
            shares[slot, piece].wait_recv()

    tile = 256 if hidden % 256 == 0 else LANES

    def expert_rows(first, count):
        rows = pl.ds(2 * first * block, 2 * count * block)
        marks = xall[rows, pl.ds(feature, width - feature)].astype(jnp.float32)
        lane = lax.broadcasted_iota(jnp.int32, marks.shape, 1)
        mine = jnp.logical_or(lane == me, lane == me + groups)
        coef = jnp.sum(jnp.where(mine, marks, 0.0), axis=1, keepdims=True)

        def body(t, carry):
            columns = pl.ds(pl.multiple_of(t * tile, tile), tile)
            values = xall[rows, pl.ds(0, feature)]
            gate = jnp.dot(values, wg[:, columns], preferred_element_type=jnp.float32)
            up = jnp.dot(values, wu[:, columns], preferred_element_type=jnp.float32)
            out = (gate / (1.0 + jnp.exp(-gate)) * up * coef).astype(jnp.bfloat16)
            for slot in range(count):
                for which in range(2):
                    start = (2 * slot + which) * block
                    hid[pl.ds(which * side + (first + slot) * block, block), columns] = out[
                        start : start + block
                    ]
            return carry

        lax.fori_loop(0, hidden // tile, body, 0)

    for step in range(1, half + 1):
        if step > 1:
            for way in range(2):
                crossed(slot_of(way, step - 1))
        for piece in range(PIECES):
            for way in range(2):
                if (way, step, piece) in hops:
                    hops[way, step, piece].wait_recv()
                    if (way, step + 1, piece) in hops:
                        hops[way, step + 1, piece].start()
                    if piece == 0:
                        crosses[slot_of(way, step)].start()
                    shares[slot_of(way, step), piece].start()
        if step == 1:
            for pieces in loads[:2]:
                for piece in pieces:
                    piece.wait()
            for piece in loads[2]:
                piece.start()
            shared(0)
            expert_rows(0, 1)
        else:
            shared(2 * step - 3)
            shared(2 * step - 2)
            expert_rows(2 * step - 3, 2)
    crossed(chips - 1)
    shared(chips - 1)
    expert_rows(chips - 1, 1)
    for piece in loads[2]:
        piece.wait()

    span = feature // CHUNKS
    part_tile = 256 if span % 256 == 0 else LANES

    last = CHUNKS - 1
    starts = [(1 - plane) * (last * span)] + [k * span for k in range(1, last)] + [plane * (last * span)]

    def at(chunk, offset, count):
        begin = starts[chunk] + offset
        if chunk in (0, last):
            begin = pl.multiple_of(begin, LANES)
        return pl.ds(begin, count)

    def project(chunk, which):
        def body(t, carry):
            columns = pl.ds(pl.multiple_of(starts[chunk] + t * part_tile, part_tile), part_tile)
            part[pl.ds(which * side, side), columns] = jnp.dot(
                hid[pl.ds(which * side, side), :], wd[:, columns],
                preferred_element_type=jnp.float32,
            ).astype(jnp.bfloat16)
            return carry

        lax.fori_loop(0, span // part_tile, body, 0)

    def area(chunk):
        return at(chunk, 0, span)

    def trade(chunk):
        return send(
            part.at[pl.ds(side, side), area(chunk)], quad.at[:, area(chunk)],
            quad_send.at[chunk], quad_recv.at[chunk], mate,
        )

    def sums(chunk, slot, offset, count):
        rows, columns = pl.ds(slot * block, block), at(chunk, offset, count)
        total = part[rows, columns].astype(jnp.float32) + quad[rows, columns].astype(jnp.float32)
        if chunk == last:
            total = total + gained[rows, pl.ds(offset, count)].astype(jnp.float32)
        return total

    def give(slot):
        rows = pl.ds(slot * block, block)
        return send(
            gift.at[rows], gained.at[rows], gift_send.at[slot], gift_recv.at[slot], twin
        )

    def lot(way, reach):
        return pl.ds((way * half + reach - 1) * block, block)

    def ship(chunk, way, reach):
        columns = area(chunk)
        if reach == half:
            columns = at(chunk, way * (span // 2), span // 2)
        index = (way * half + reach - 1) * CHUNKS + chunk
        return send(
            outgo.at[lot(way, reach), columns], income.at[lot(way, reach), columns],
            rs_send.at[index], rs_recv.at[index], sides[way],
        )

    def swap(chunk):
        return send(
            fin.at[:, area(chunk)], other.at[:, area(chunk)],
            dp_send.at[chunk], dp_recv.at[chunk], twin,
        )

    gifts = [give(slot) for slot in range(chips)]
    trades = [trade(chunk) for chunk in range(CHUNKS)]
    swaps = {chunk: swap(chunk) for chunk in range(1, CHUNKS)}
    ships = {
        (chunk, way, reach): ship(chunk, way, reach)
        for chunk in range(1, CHUNKS) for way in range(2) for reach in range(1, half + 1)
    }

    def stage(chunk, number):
        if number == 0:
            project(chunk, 1)
            trades[chunk].start()
            project(chunk, 0)
        elif number == 1 and chunk == 0:
            trades[chunk].wait_recv()
            for slot in reversed(range(chips)):
                gift[pl.ds(slot * block, block), :] = sums(0, slot, 0, span).astype(jnp.bfloat16)
                gifts[slot].start()
        elif chunk == 0:
            pass
        elif number == 1:
            trades[chunk].wait_recv()
            if chunk == last:
                gifts[chips - 1].wait_recv()
            for way in range(2):
                columns = at(chunk, way * (span // 2), span // 2)
                total = sums(chunk, chips - 1, way * (span // 2), span // 2)
                outgo[lot(way, half), columns] = total.astype(jnp.bfloat16)
                ships[chunk, way, half].start()
        elif number <= half:
            reach = half + 1 - number
            for way in range(2):
                ships[chunk, way, reach + 1].wait_recv()
                slot = 2 * reach - way
                if chunk == last:
                    gifts[slot].wait_recv()
                for piece in range(2):
                    columns = at(chunk, piece * (span // 2), span // 2)
                    total = sums(chunk, slot, piece * (span // 2), span // 2)
                    if reach + 1 < half or piece == way:
                        total = total + income[lot(way, reach + 1), columns].astype(jnp.float32)
                    outgo[lot(way, reach), columns] = total.astype(jnp.bfloat16)
                ships[chunk, way, reach].start()
        elif number == half + 1:
            ships[chunk, 0, 1].wait_recv()
            ships[chunk, 1, 1].wait_recv()
            columns = area(chunk)
            if chunk == last:
                gifts[0].wait_recv()
            total = sums(chunk, 0, 0, span)
            total = total + income[lot(0, 1), columns].astype(jnp.float32)
            total = total + income[lot(1, 1), columns].astype(jnp.float32)
            fin[:, columns] = total.astype(jnp.bfloat16)
            swaps[chunk].start()
        else:
            swaps[chunk].wait_recv()
            columns = area(chunk)
            if chunk == last:
                o_ref[:, columns] = fin[:, columns]
                o_ref[:, area(0)] = other[:, area(0)]
                return
            o_ref[:, columns] = (
                fin[:, columns].astype(jnp.float32) + other[:, columns].astype(jnp.float32)
            ).astype(jnp.bfloat16)

    stages = half + 3
    for wave in range(CHUNKS + stages - 1):
        if wave < CHUNKS:
            stage(wave, 0)
        for chunk in range(CHUNKS):
            if 0 < wave - chunk < stages:
                stage(chunk, wave - chunk)

    copies = list(hops.values()) + list(shares.values()) + trades
    for copy in copies + list(crosses.values()) + gifts + list(swaps.values()) + list(ships.values()):
        copy.wait_send()


def ring_form(tokens, expert_ids, gate_ints, w_gate, w_up, w_down):
    groups = lax.axis_size("expert")
    chips, half = groups // 2, groups // 4
    block, feature = tokens.shape
    hidden = w_gate.shape[2]
    marks = -(-2 * groups // LANES) * LANES
    width = feature + marks
    rows = groups * block
    dma = pltpu.SemaphoreType.DMA
    return pl.pallas_call(
        functools.partial(ring_kernel, groups),
        out_shape=jax.ShapeDtypeStruct((block, feature), jnp.bfloat16),
        in_specs=[
            pl.BlockSpec(memory_space=pl.ANY),
            pl.BlockSpec(memory_space=pltpu.VMEM),
            pl.BlockSpec(memory_space=pltpu.VMEM),
        ]
        + [pl.BlockSpec(memory_space=pl.ANY)] * 3,
        out_specs=pl.BlockSpec(memory_space=pltpu.VMEM),
        scratch_shapes=[
            pltpu.VMEM((rows, width), jnp.bfloat16),
            pltpu.VMEM((feature, hidden), jnp.bfloat16),
            pltpu.VMEM((feature, hidden), jnp.bfloat16),
            pltpu.VMEM((hidden, feature), jnp.bfloat16),
            pltpu.VMEM((rows, hidden), jnp.bfloat16),
            pltpu.VMEM((rows, feature), jnp.bfloat16),
            pltpu.VMEM((chips * block, feature), jnp.bfloat16),
            pltpu.VMEM((2 * half * block, feature), jnp.bfloat16),
            pltpu.VMEM((2 * half * block, feature), jnp.bfloat16),
            pltpu.VMEM((block, feature), jnp.bfloat16),
            pltpu.VMEM((block, feature), jnp.bfloat16),
            pltpu.VMEM((chips * block, feature // CHUNKS), jnp.bfloat16),
            pltpu.VMEM((chips * block, feature // CHUNKS), jnp.bfloat16),
            dma((3 * WEIGHT_PIECES,)),
            dma,
            dma((2 * half * PIECES,)),
            dma((2 * half * PIECES,)),
            dma((chips * PIECES,)),
            dma((chips * PIECES,)),
            dma((CHUNKS,)),
            dma((CHUNKS,)),
            dma((2 * half * CHUNKS,)),
            dma((2 * half * CHUNKS,)),
            dma((CHUNKS,)),
            dma((CHUNKS,)),
            dma((chips,)),
            dma((chips,)),
            dma((chips,)),
            dma((chips,)),
        ],
        compiler_params=pltpu.CompilerParams(
            collective_id=0, has_side_effects=True, vmem_limit_bytes=60 * 1024 * 1024
        ),
    )(tokens, expert_ids, gate_ints, w_gate, w_up, w_down)


def dispatch_form(tokens, expert_ids, gate_ints, w_gate, w_up, w_down):
    tok_rows = tokens.shape[0]
    top_count = expert_ids.shape[1]
    feature = tokens.shape[1]
    groups = lax.axis_size("expert")
    capacity = min(tok_rows, max(2, 3 * tok_rows * top_count // (2 * groups)))
    pairs = tok_rows * top_count
    flat_ids = expert_ids.reshape(pairs)
    onehot = (flat_ids[:, None] == jnp.arange(groups, dtype=jnp.int32)[None, :]).astype(jnp.int32)
    before = jnp.cumsum(onehot, axis=0) - onehot
    slot = jnp.sum(before * onehot, axis=1)
    target = flat_ids * capacity + slot
    select = (jnp.arange(groups * capacity, dtype=jnp.int32)[:, None] == target[None, :]).astype(
        jnp.bfloat16
    )
    owner = (
        (jnp.arange(pairs, dtype=jnp.int32) // top_count)[:, None]
        == jnp.arange(tok_rows, dtype=jnp.int32)[None, :]
    ).astype(jnp.bfloat16)
    placing = jnp.dot(select, owner, preferred_element_type=jnp.float32).astype(jnp.bfloat16)
    outgoing = jnp.dot(placing, tokens, preferred_element_type=jnp.float32).astype(jnp.bfloat16)
    arrived = lax.all_to_all(
        outgoing.reshape(groups, capacity, feature),
        "expert",
        split_axis=0,
        concat_axis=0,
        tiled=True,
    )
    rows = arrived.reshape(groups * capacity, feature)
    gate = jnp.dot(rows, w_gate[0], preferred_element_type=jnp.float32)
    up = jnp.dot(rows, w_up[0], preferred_element_type=jnp.float32)
    hidden = (jax.nn.silu(gate) * up).astype(jnp.bfloat16)
    partial_value = jnp.dot(hidden, w_down[0], preferred_element_type=jnp.float32).astype(
        jnp.bfloat16
    )
    back = lax.all_to_all(
        partial_value.reshape(groups, capacity, feature),
        "expert",
        split_axis=0,
        concat_axis=0,
        tiled=True,
    )
    back_rows = back.reshape(groups * capacity, feature)
    weights = (gate_ints.astype(jnp.float32) / 1024.0)[:, :, None]
    picked = (
        jnp.take(back_rows, target, axis=0)
        .reshape(tok_rows, top_count, feature)
        .astype(jnp.float32)
    )
    local_mix = jnp.sum(weights * picked, axis=1)
    mixed = lax.psum(local_mix.astype(jnp.bfloat16), "dp")
    return mixed


def on_device(tokens, expert_ids, *rest):
    tok_rows, top_count = expert_ids.shape
    groups = lax.axis_size("expert")
    capacity = min(tok_rows, max(2, 3 * tok_rows * top_count // (2 * groups)))
    fits = groups % 4 == 0 and groups >= 8 and lax.axis_size("dp") == 2
    form = ring_form if fits and tok_rows <= 2 * capacity else dispatch_form
    return form(tokens, expert_ids, *rest)


def solution(mesh):
    return jax.shard_map(
        on_device,
        mesh=mesh,
        in_specs=(
            P("expert", None),
            P("expert", None),
            P("expert", None),
            P("expert", None, "dp"),
            P("expert", None, "dp"),
            P("expert", "dp", None),
        ),
        out_specs=P("expert", None),
        check_vma=False,
    )
```
